128 devices in a mesh: lon: 32 (over y, z, x_lo), chan: 4 (over x_hi, core).
Axes of the slice: x: 4 (x_hi: 2, x_lo: 2; x = x_hi * 2 + x_lo), y: 4, z: 4, core: 2. Of those that a mesh axis runs over, the one named last changes fastest.
Arguments:
- fields: bfloat16 [1440, 49152], P('lon', 'chan'), may hold values from -6 to 6
- mix_weight: bfloat16 [384, 3456], P('chan'), may hold values from -0.109375 to 0.109375
- basis_values: float32 [5, 9, 65, 128], replicated, may hold values from -0.4 to 0.4
- source_rows: int32 [128, 5], replicated, may hold values from 0 to 131, as said below
- lon_reach: int32 [128, 5], replicated, may hold values from 1 to 32, as said below
- quad_weights: float32 [128], replicated, may hold values from 0.2 to 2
Outputs:
- spectrum: float32 [128, 552960], P('lon', 'chan')
The draws below stay inside these ranges and needn't reach their ends.
Inputs may be any that keep to these rules, and one draw needn't show every extreme that they name: source_rows[i, e] lies between i + 4 - 4 and i + 8; entry 0 of row i is i + 4 and entry 1 is i + 4 - 4. `lon_reach`: every entry of the rows under 4 has reach 32.
All inputs are finite; a program needn't handle non-finite values.
Results may differ from the reference program's by a relative error of at most 0.005.
Values may be sent and summed in bfloat16 or wider, within the bound.
A program may use at most 128 MiB of HBM per device.

```python
import math
import jax
import jax.numpy as jnp
from jax import lax

C = 384
NLON = 1440
MODES = 720
K = 9
NNZ = 5
H = 32
POLE = 4
RR = 4
LAT = 128


def draw_source_rows(key, part):
    own_rows = jnp.arange(LAT, dtype=jnp.int32)[:, None] + POLE
    offsets = jax.random.randint(key, (LAT, NNZ - 2), -RR, RR + 1)
    others = jnp.minimum(own_rows + offsets, LAT + POLE - 1)
    return jnp.concatenate([own_rows, own_rows - RR, others], axis=1).astype(jnp.int32)


def draw_lon_reach(key, part):
    drawn = jax.random.randint(key, (LAT, NNZ), 1, H + 1)
    polar = jnp.arange(LAT, dtype=jnp.int32)[:, None] < POLE
    return jnp.where(polar, jnp.full_like(drawn, H), drawn).astype(jnp.int32)


def shard_levels(key, shape, split, smallest, high):
    def one(axis_at, parts):
        steps = jax.random.uniform(jax.random.fold_in(jax.random.fold_in(key, 6), axis_at), (parts,), jnp.float32, smallest / len(split), high / len(split))
        return jnp.repeat(jnp.exp(steps), shape[axis_at] // parts).reshape((-1,) + (1,) * (len(shape) - axis_at - 1))

    gain = one(*split[0])
    for cut in split[1:]:
        gain = gain * one(*cut)
    return gain


def bell_draw(key, shape, scale, bound, shards=(), kind=jnp.bfloat16):
    values = jax.random.normal(key, shape, jnp.float32) * scale
    if len(shards) > 0:
        values = shard_levels(key, shape, shards, -0.22, 0.18) * values
    return jnp.clip(values, min=-bound, max=bound).astype(kind)


def setup_inputs(seed: int = 0) -> dict:
    streams_of = jax.random.split(jax.random.key(seed), 7)
    return {
        "fields": bell_draw(streams_of[0], (NLON, C * LAT), 1.0, 6.0, ((0, 32), (1, 4))),
        "mix_weight": bell_draw(streams_of[1], (C, K * C), (K * C) ** -0.5, 0.109375, ((0, 4),)),
        "basis_values": bell_draw(streams_of[2], (NNZ, K, 2 * H + 1, LAT), 0.06, 0.4, (), jnp.float32),
        "source_rows": draw_source_rows(jax.random.fold_in(streams_of[6], 71), 0),
        "lon_reach": draw_lon_reach(jax.random.fold_in(streams_of[6], 71), 0),
        "quad_weights": jnp.clip(jnp.exp(jax.random.uniform(streams_of[5], (LAT,), jnp.float32, math.log(0.2), math.log(2.0))), 0.2, 2.0),
    }


def reference(fields, mix_weight, basis_values, source_rows, lon_reach, quad_weights):
    half_turn = NLON // 2
    grid = fields.reshape(NLON, C, LAT).transpose(2, 0, 1)
    images = jnp.roll(grid[:POLE], -half_turn, axis=1)[::-1]
    extended = jnp.concatenate([images, grid], axis=0)
    padded = jnp.concatenate([extended[:, NLON - H:], extended, extended[:, :H]], axis=1)
    quad_ext = jnp.concatenate([quad_weights[:POLE][::-1], quad_weights], axis=0)
    row_quad = jnp.take(quad_ext, source_rows, axis=0)
    offsets = jnp.arange(2 * H + 1, dtype=jnp.int32) - H
    keeping = jnp.abs(offsets)[None, None, :] <= lon_reach[:, :, None]
    basis_rows = basis_values.transpose(3, 0, 1, 2)
    weighted = basis_rows * row_quad[:, :, None, None]
    filters = jnp.where(keeping[:, :, None, :], weighted, jnp.zeros_like(weighted)).astype(jnp.bfloat16)
    weight_full = mix_weight.reshape(C, K, C).transpose(1, 2, 0).astype(jnp.float32)

    def one_row(index):
        picked = jnp.take(padded, source_rows[index], axis=0)
        row_filter = filters[index].astype(jnp.float32)
        total = jnp.zeros((K, NLON, C), jnp.float32)
        for shift_index in range(2 * H + 1):
            window = picked[:, shift_index:shift_index + NLON].astype(jnp.float32)
            total = total + jnp.einsum('ejc,ek->kjc', window, row_filter[:, :, shift_index])
        filtered = total.astype(jnp.bfloat16).astype(jnp.float32)
        return jnp.einsum('kjc,kco->jo', filtered, weight_full).astype(jnp.bfloat16)

    mixed = lax.map(one_row, jnp.arange(LAT, dtype=jnp.int32))
    trans = jnp.fft.rfft(mixed.astype(jnp.float32), axis=1, norm="ortho")[:, :MODES]
    real_part = jnp.real(trans).transpose(0, 2, 1)
    imag_part = jnp.imag(trans).transpose(0, 2, 1)
    stacked = jnp.stack([real_part, imag_part], axis=2)
    return stacked.reshape(LAT, C * 2 * MODES).astype(jnp.float32)
```

```python
import functools
import math

import jax
import jax.numpy as jnp
import numpy as np
from jax import lax
from jax.experimental import pallas as pl
from jax.experimental.pallas import tpu as pltpu
from jax.sharding import Mesh, PartitionSpec as P

C = 384
MODES = 720
NLON = 1440
K = 9
NNZ = 5
POLE = 4
LINE = 8
PLANE = 16
ROWS = 16
SPAN = 24
SLAB = 45
OWN = 96
PAD = 48
WIDTH = 90
TILE = 48
EXT = 176
MESH = pl.DeviceIdType.MESH


def place():
    y, z = lax.axis_index("y"), lax.axis_index("z")
    xlo, chan = lax.axis_index("xlo"), lax.axis_index("chan")
    return y, z, xlo, chan, y * 4 + z, xlo * 4 + chan


def remote(src, dst, send, recv, where):
    return pltpu.make_async_remote_copy(
        src_ref=src, dst_ref=dst, send_sem=send, recv_sem=recv, device_id=where, device_id_type=MESH
    )


def gather_kernel(
    fields_ref, weight_ref, basis_ref, quad_ref, reach_ref,
    got_ref, halo_ref, whole_ref, filt_ref,
    wide_ref, rows_ref, tmp_ref,
    line_send, line_recv, cap_send, cap_recv, halo_send, halo_recv,
    part_send, part_recv, pair_send, pair_recv, fan_send, fan_recv, own_sem,
):
    y, z, xlo, chan, yz, me = place()
    at_line = lambda p: (y, z, p // 4, lax.rem(p, 4))
    at_plane = lambda p: (p // 4, lax.rem(p, 4), xlo, chan)
    barrier = pltpu.get_barrier_semaphore()
    for d in range(1, LINE):
        pl.semaphore_signal(barrier, inc=1, device_id=at_line(lax.rem(me + d, LINE)), device_id_type=MESH)
    for d in range(1, PLANE):
        pl.semaphore_signal(barrier, inc=1, device_id=at_plane(lax.rem(yz + d, PLANE)), device_id_type=MESH)
    pl.semaphore_wait(barrier, LINE + PLANE - 2)

    other = lax.rem(chan + 2, 4)
    twin = chan + 1 - 2 * lax.rem(chan, 2)
    far = lax.rem(twin + 2, 4)
    mine = pltpu.make_async_copy(weight_ref, whole_ref.at[chan], own_sem.at[0])
    mine.start()
    to_twin = remote(weight_ref, whole_ref.at[chan], pair_send.at[0], pair_recv.at[0], (y, z, xlo, twin))
    to_twin.start()
    piece = pl.ds(pl.multiple_of(lax.rem(yz, K) * C, 128), C)
    across = remote(
        weight_ref.at[:, piece], whole_ref.at[chan, :, piece], part_send, part_recv, (y, z, 1 - xlo, other)
    )

    @pl.when(yz < K)
    def _():
        across.start()

    shift = POLE * PAD + 3 * xlo
    zeros = jnp.zeros((128 - OWN, 128), jnp.float32)
    for l in range(SLAB):
        turned = jnp.concatenate([fields_ref[l].astype(jnp.float32), zeros], axis=0).T
        wide_ref[pl.ds(shift + l, 128, stride=PAD), :] = turned

    def narrow(row, carry):
        at = pl.multiple_of(row * PAD, PAD)
        rows_ref[row] = wide_ref[pl.ds(at, PAD), :].astype(jnp.bfloat16)
        return carry

    lax.fori_loop(POLE, POLE + 128, narrow, 0, unroll=4)
    rows_ref[POLE + 128 :] = jnp.zeros((POLE, PAD, 128), jnp.bfloat16)

    caps = [
        remote(
            rows_ref.at[POLE + g], rows_ref.at[POLE - 1 - g], cap_send.at[g], cap_recv.at[g],
            (lax.rem(y + 2, 4), z, xlo, chan),
        )
        for g in range(POLE)
    ]
    for copy in caps:
        copy.start()

    def line_copy(peer):
        span = rows_ref.at[pl.ds(pl.multiple_of(peer * ROWS, ROWS), SPAN)]
        return remote(span, got_ref.at[me], line_send.at[peer], line_recv.at[me], at_line(peer))

    for d in range(1, LINE):
        peer = lax.rem(me + d, LINE)

        @pl.when(peer != 0)
        def _():
            line_copy(peer).start()

    for copy in caps:
        copy.wait()

    @pl.when(me != 0)
    def _():
        line_copy(0).start()

    own = pltpu.make_async_copy(
        rows_ref.at[pl.ds(pl.multiple_of(me * ROWS, ROWS), SPAN)], got_ref.at[me], own_sem.at[1]
    )
    own.start()

    def fan_copy(source, target):
        part = pl.ds(pl.multiple_of(source * C, 128), C)
        return remote(
            whole_ref.at[other, :, part], whole_ref.at[other, :, part],
            fan_send.at[target], fan_recv.at[source], at_plane(target),
        )

    @pl.when(yz < K)
    def _():
        across.wait()
        for d in range(1, PLANE):
            fan_copy(yz, lax.rem(yz + d, PLANE)).start()

    def one_filter(index, carry):
        e = index // K
        k = lax.rem(index, K)
        tall = jnp.concatenate(
            [basis_ref[e, k], jnp.zeros((128 - 65, 128), jnp.float32)], axis=0
        )
        tmp_ref[...] = tall.T
        taps = tmp_ref[pl.ds(pl.multiple_of(me * ROWS, ROWS), ROWS), :]
        quads = quad_ref[e]
        reach = reach_ref[e]
        away = jnp.abs(lax.broadcasted_iota(jnp.int32, (ROWS, 128), 1) - 32)
        kept = jnp.where(away <= reach, taps * quads, 0.0)
        kept = kept.astype(jnp.bfloat16).astype(jnp.float32)
        filt_ref[pl.ds(index, ROWS, stride=TILE), :] = kept
        return carry

    lax.fori_loop(0, NNZ * K, one_filter, 0)

    def halo_copy(slot):
        side = slot // 4
        source = got_ref.at[slot, :, pl.ds(pl.multiple_of(side * 16, 16), 32)]
        target = lax.rem(yz + PLANE - 1 + 2 * side, PLANE)
        return remote(source, halo_ref.at[slot], halo_send.at[slot], halo_recv.at[slot], at_plane(target))

    own.wait()
    halo_copy(me).start()
    for d in range(1, LINE):
        slot = lax.rem(me + LINE - d, LINE)
        remote(
            rows_ref.at[pl.ds(0, SPAN)], got_ref.at[slot], line_send.at[slot], line_recv.at[slot], at_line(slot)
        ).wait_recv()
        halo_copy(slot).start()

    for source in range(K):

        @pl.when(yz != source)
        def _():
            fan_copy(source, yz).wait_recv()

    far_copy = remote(
        whole_ref.at[other], whole_ref.at[other], pair_send.at[1], pair_recv.at[1], (y, z, xlo, twin)
    )
    far_copy.start()
    for slot in range(LINE):
        halo_copy(slot).wait()
    far_copy.wait()
    to_twin.wait()
    mine.wait()
    for d in range(1, LINE):
        line_copy(lax.rem(me + d, LINE)).wait_send()

    @pl.when(yz < K)
    def _():
        for d in range(1, PLANE):
            fan_copy(yz, lax.rem(yz + d, PLANE)).wait_send()


def gather(fields, weight, basis, quads, reach):
    vmem = pl.BlockSpec(memory_space=pltpu.VMEM)
    hbm = pl.BlockSpec(memory_space=pl.ANY)
    dma = pltpu.SemaphoreType.DMA
    return pl.pallas_call(
        gather_kernel,
        out_shape=(
            jax.ShapeDtypeStruct((LINE, SPAN, PAD, 128), jnp.bfloat16),
            jax.ShapeDtypeStruct((LINE, SPAN, 32, 128), jnp.bfloat16),
            jax.ShapeDtypeStruct((4, OWN, K * C), jnp.bfloat16),
            jax.ShapeDtypeStruct((ROWS * TILE, 128), jnp.float32),
        ),
        in_specs=[vmem] * 5,
        out_specs=(hbm, hbm, hbm, vmem),
        scratch_shapes=[
            pltpu.VMEM(((128 + 2 * POLE) * PAD, 128), jnp.float32),
            pltpu.VMEM((128 + 2 * POLE, PAD, 128), jnp.bfloat16),
            pltpu.VMEM((128, 128), jnp.float32),
            dma((LINE,)), dma((LINE,)), dma((POLE,)), dma((POLE,)), dma((LINE,)), dma((LINE,)),
            dma, dma, dma((2,)), dma((2,)), dma((PLANE,)), dma((PLANE,)), dma((2,)),
        ],
        compiler_params=pltpu.CompilerParams(
            collective_id=0, has_side_effects=True, vmem_limit_bytes=48 << 20
        ),
    )(fields, weight, basis, quads, reach)


def layer_kernel(
    src_ref, filt_ref, got_ref, halo_ref, w_ref, p_ref, q_ref, u_ref, v_ref,
    out_ref,
    flat_ref, x_ref, band_ref, filtered_ref, sent_ref, all_ref, table_ref,
    send_sem, recv_sem, own_sem,
):
    y, z, xlo, chan, yz, me = place()
    source = 2 * y + z // 2
    barrier = pltpu.get_barrier_semaphore()

    def is_self(b):
        return jnp.logical_and(b == yz, source == me)

    for b in range(PLANE):

        @pl.when(jnp.logical_not(is_self(b)))
        def _():
            pl.semaphore_signal(
                barrier, inc=1, device_id=(b // 4, b % 4, source // 4, lax.rem(source, 4)), device_id_type=MESH
            )

    def lay(u, carry):
        def joined(ref, first):
            return jnp.concatenate(
                [ref[first + q, u].astype(jnp.float32)[:, :OWN] for q in range(4)], axis=1
            )

        flat_ref[0:32, :] = joined(halo_ref, 4)
        flat_ref[32:77, :] = joined(got_ref, 0)[:SLAB]
        flat_ref[77:122, :] = joined(got_ref, 4)[3:]
        flat_ref[122:154, :] = joined(halo_ref, 0)
        flat_ref[154:EXT, :] = jnp.zeros((EXT - 154, C), jnp.float32)
        x_ref[u] = flat_ref[...].astype(jnp.bfloat16)
        return carry

    lax.fori_loop(0, SPAN, lay, 0)

    targets = jnp.where(jnp.logical_and(y == me // 2, z // 2 == lax.rem(me, 2)), PLANE - 1, PLANE)
    pl.semaphore_wait(barrier, targets)

    def target_of(s):
        return me // 2, lax.rem(me, 2) * 2 + s // 2, lax.rem(s, 2)

    def send_copy(s, o):
        ty, tz, tx = target_of(s)
        return remote(
            sent_ref.at[s, o], all_ref.at[yz], send_sem.at[s, o], recv_sem.at[yz], (ty, tz, tx, o)
        )

    def own_copy(s, o):
        return pltpu.make_async_copy(sent_ref.at[s, o], all_ref.at[yz], own_sem)

    def to_self(s, o):
        ty, tz, tx = target_of(s)
        return (ty == y) & (tz == z) & (tx == xlo) & (chan == o)

    first = lax.rem(2 * z + xlo, 4)

    def one_group(step, carry):
        s = lax.rem(step + first, 4)

        def one_row(sub, carry):
            row = s * 4 + sub
            for k in range(K):
                for e in range(NNZ):
                    taps = filt_ref[pl.ds(row * TILE + e * K + k, 1), :]
                    spread = jnp.broadcast_to(taps, (TILE, 128))
                    rolled = pltpu.roll(spread, 0, 1, stride=1, stride_axis=0)
                    band_ref[pl.ds(k * TILE, TILE), pl.ds(e * 128, 128)] = rolled.astype(jnp.bfloat16)
            for half in range(2):
                window = jnp.concatenate(
                    [x_ref[src_ref[row, e], pl.ds(half * TILE, 128), :] for e in range(NNZ)], axis=0
                )
                total = jnp.dot(band_ref[...], window, preferred_element_type=jnp.float32)
                rounded = total.astype(jnp.bfloat16)
                at = pl.multiple_of(sub * (2 * TILE) + half * TILE, 16)
                for k in range(K):
                    filtered_ref[k, pl.ds(at, TILE), :] = rounded[k * TILE : (k + 1) * TILE]
            return carry

        lax.fori_loop(0, 4, one_row, 0)
        acc = jnp.zeros((4 * 2 * TILE, C), jnp.float32)
        for k in range(K):
            acc += lax.dot_general(
                filtered_ref[k],
                w_ref[:, k * C : (k + 1) * C],
                (((1,), (1,)), ((), ())),
                preferred_element_type=jnp.float32,
            )
        for o in range(4):
            piece = jnp.concatenate(
                [acc[i * 96 : (i + 1) * 96, o * OWN : (o + 1) * OWN] for i in range(4)], axis=1
            )
            sent_ref[s, o] = piece.astype(jnp.bfloat16)
        for o in range(4):

            @pl.when(to_self(s, o))
            def _():
                own_copy(s, o).start()

            @pl.when(jnp.logical_not(to_self(s, o)))
            def _():
                send_copy(s, o).start()

        return carry

    lax.fori_loop(0, 4, one_group, 0)

    def one_table(b, carry):
        at = pl.multiple_of(b * 96, 96)
        part = u_ref[pl.ds(b, 1), :] * p_ref[...] + v_ref[pl.ds(b, 1), :] * q_ref[...]
        table_ref[pl.ds(at, 96), :] = part.astype(jnp.bfloat16)
        return carry

    lax.fori_loop(0, PLANE, one_table, 0)

    for s in range(4):
        for o in range(4):

            @pl.when(to_self(s, o))
            def _():
                own_copy(s, o).wait()

            @pl.when(jnp.logical_not(to_self(s, o)))
            def _():
                send_copy(s, o).wait_send()

    for b in range(PLANE):

        @pl.when(jnp.logical_not(is_self(b)))
        def _():
            remote(
                sent_ref.at[0, 0], all_ref.at[b], send_sem.at[0, 0], recv_sem.at[b], (b // 4, b % 4, xlo, chan)
            ).wait_recv()

    block = all_ref[...].reshape(PLANE * 96, C)
    out_ref[...] = lax.dot_general(
        block, table_ref[...], (((0,), (0,)), ((), ())), preferred_element_type=jnp.float32
    )


def layer(src, filt, got, halo, weight, tables):
    vmem = pl.BlockSpec(memory_space=pltpu.VMEM)
    dma = pltpu.SemaphoreType.DMA
    return pl.pallas_call(
        layer_kernel,
        out_shape=jax.ShapeDtypeStruct((C, 2 * MODES), jnp.float32),
        in_specs=[pl.BlockSpec(memory_space=pltpu.SMEM)] + [vmem] * 8,
        out_specs=vmem,
        scratch_shapes=[
            pltpu.VMEM((EXT, C), jnp.float32),
            pltpu.VMEM((SPAN, EXT, C), jnp.bfloat16),
            pltpu.VMEM((K * TILE, NNZ * 128), jnp.bfloat16),
            pltpu.VMEM((K, 4 * 2 * TILE, C), jnp.bfloat16),
            pltpu.VMEM((4, 4, 96, C), jnp.bfloat16),
            pltpu.VMEM((PLANE, 96, C), jnp.bfloat16),
            pltpu.VMEM((PLANE * 96, 2 * MODES), jnp.bfloat16),
            dma((4, 4)), dma((PLANE,)), dma,
        ],
        compiler_params=pltpu.CompilerParams(
            collective_id=1, has_side_effects=True, vmem_limit_bytes=56 << 20
        ),
    )(src, filt, got, halo, weight, *tables)


def dft_parts():
    modes = np.arange(MODES)
    high = 2 * math.pi * ((np.arange(PLANE)[:, None] * WIDTH * modes[None]) % NLON) / NLON
    low = 2 * math.pi * ((np.arange(96)[:, None] * modes[None]) % NLON) / NLON
    factor = 1 / math.sqrt(NLON)
    inside = (np.arange(96) < WIDTH)[:, None]
    ca, sa = np.cos(high) * factor, np.sin(high) * factor
    cb, sb = np.cos(low) * inside, np.sin(low) * inside
    side = lambda a, b: jnp.asarray(np.concatenate([a, b], axis=1), jnp.float32)
    return side(cb, cb), side(sb, sb), side(ca, -sa), side(-sa, -ca)


def shards(fields, mix_weight, basis_values, source_rows, lon_reach, quad_weights):
    start = lax.axis_index(("xlo", "chan")) * ROWS
    quad_ext = jnp.concatenate([quad_weights[:POLE][::-1], quad_weights], axis=0)
    src = lax.dynamic_slice_in_dim(source_rows, start, ROWS, 0)
    reach = lax.dynamic_slice_in_dim(lon_reach, start, ROWS, 0)
    here = src[:, :, None] == jnp.arange(quad_ext.shape[0], dtype=jnp.int32)
    row_quad = jnp.sum(jnp.where(here, quad_ext, 0.0), axis=2)
    local = fields.reshape(SLAB, OWN, 128)
    got, halo, weight, filt = gather(
        local, mix_weight, basis_values, row_quad.T[:, :, None], reach.T[:, :, None]
    )
    out = layer(src - start, filt, got, halo, weight.reshape(C, K * C), dft_parts())
    return out.reshape(4, OWN * 2 * MODES)


def solution(mesh):
    fine = Mesh(mesh.devices.reshape(4, 4, 2, 4), ("y", "z", "xlo", "chan"))
    lon = ("y", "z", "xlo")
    placed = (P(lon, "chan"), P("chan", None), P(), P(), P(), P())
    return jax.shard_map(
        shards, mesh=fine, in_specs=placed, out_specs=P(lon, "chan"), check_vma=False
    )
```

```python
import functools
import math

import jax
import jax.numpy as jnp
import numpy as np
from jax import lax
from jax.experimental import pallas as pl
from jax.experimental.pallas import tpu as pltpu
from jax.sharding import Mesh, PartitionSpec as P

C = 384
MODES = 720
NLON = 1440
K = 9
NNZ = 5
POLE = 4
LINE = 8
PLANE = 16
ROWS = 16
SPAN = 24
SLAB = 45
OWN = 96
PAD = 48
WIDTH = 90
TILE = 32
EXT = 160
TAPS = 80
PARTS = 6
MESH = pl.DeviceIdType.MESH


def place():
    y, z = lax.axis_index("y"), lax.axis_index("z")
    xlo, chan = lax.axis_index("xlo"), lax.axis_index("chan")
    return y, z, xlo, chan, y * 4 + z, xlo * 4 + chan


def remote(src, dst, send, recv, where):
    return pltpu.make_async_remote_copy(
        src_ref=src, dst_ref=dst, send_sem=send, recv_sem=recv, device_id=where, device_id_type=MESH
    )


def layer_kernel(
    src_ref, reach_ref, quad_ref, fields_ref, weight_ref, basis_in, p_in, q_in, u_in, v_in,
    out_ref,
    basis_ref, p_ref, q_ref, u_ref, v_ref, load_sem,
    tall_ref, wide_ref, rows_ref, tmp_ref, got_ref, edge_ref, halo_ref, land_ref, whole_ref, filt_ref, flat_ref, x_ref,
    even_ref, odd_ref, filtered_ref, sent_ref, all_ref, table_ref, result_ref,
    line_send, line_recv, cap_send, cap_recv, halo_send, halo_recv,
    part_send, part_recv, pair_send, pair_recv, fan_z_send, fan_z_recv, fan_y_send, fan_y_recv, own_sem,
    send_sem, recv_sem, ready_sem, stage_ref, out_sem,
):
    y, z, xlo, chan, yz, me = place()
    at_line = lambda p: (y, z, p // 4, lax.rem(p, 4))
    at_plane = lambda p: (p // 4, lax.rem(p, 4), xlo, chan)
    source = 2 * y + z // 2
    barrier = pltpu.get_barrier_semaphore()

    def signal(where):
        pl.semaphore_signal(barrier, inc=1, device_id=where, device_id_type=MESH)

    for d in range(1, LINE):
        signal(at_line(lax.rem(me + d, LINE)))
    for d in range(1, PLANE):
        signal(at_plane(lax.rem(yz + d, PLANE)))
    loads = [
        pltpu.make_async_copy(a, b, load_sem.at[i])
        for i, (a, b) in enumerate(
            [(basis_in, basis_ref), (p_in, p_ref), (q_in, q_ref), (u_in, u_ref), (v_in, v_ref)]
        )
    ]
    for copy in loads:
        copy.start()

    for c in range(OWN):
        tall_ref[c * PAD : c * PAD + SLAB, :] = fields_ref[:, c * 128 : (c + 1) * 128].astype(jnp.float32)
    shift = POLE * PAD + 3 * xlo
    zeros = jnp.zeros((128 - OWN, 128), jnp.float32)
    for l in range(SLAB):
        turned = jnp.concatenate([tall_ref[pl.ds(l, OWN, stride=PAD), :], zeros], axis=0).T
        wide_ref[pl.ds(shift + l, 128, stride=PAD), :] = turned

    def narrow(row, carry):
        at = pl.multiple_of(row * PAD, PAD)
        rows_ref[row] = wide_ref[pl.ds(at, PAD), :].astype(jnp.bfloat16)
        return carry

    lax.fori_loop(POLE, POLE + 128, narrow, 0, unroll=4)
    rows_ref[POLE + 128 :] = jnp.zeros((POLE, PAD, 128), jnp.bfloat16)

    pl.semaphore_wait(barrier, LINE + PLANE - 2)
    for d in range(1, LINE):
        pl.semaphore_signal(
            ready_sem, inc=1, device_id=at_line(lax.rem(me + d, LINE)), device_id_type=MESH
        )

    caps = [
        remote(
            rows_ref.at[POLE + g], rows_ref.at[POLE - 1 - g], cap_send.at[g], cap_recv.at[g],
            (lax.rem(y + 2, 4), z, xlo, chan),
        )
        for g in range(POLE)
    ]
    for copy in caps:
        copy.start()

    other = lax.rem(chan + 2, 4)
    twin = chan + 1 - 2 * lax.rem(chan, 2)
    part_spot = lambda p: pl.ds(pl.multiple_of(p * C, 128), C)
    owned = y + 4 * z
    piece = part_spot(lax.rem(owned, K))
    across = remote(
        weight_ref.at[:, piece], whole_ref.at[chan, :, piece], part_send, part_recv, (y, z, 1 - xlo, other)
    )

    @pl.when(owned < K)
    def _():
        across.start()

    def line_copy(peer, c):
        return remote(
            rows_ref.at[pl.ds(peer * ROWS + 4 * c, 4)], got_ref.at[me, pl.ds(4 * c, 4)],
            line_send.at[peer, c], line_recv.at[me, c], at_line(peer),
        )

    def takes(peer, c):
        return lax.rem(peer, 2) * 2 + 4 > c

    def each_line(c, act):
        for d in range(1, LINE):
            peer = lax.rem(me + d, LINE)
            if isinstance(c, int) and c < 4:
                act(peer)
            else:
                pl.when(takes(peer, c))(functools.partial(act, peer))

    for d in range(1, LINE):
        peer = lax.rem(me + d, LINE)

        @pl.when(peer != 0)
        def _():
            line_copy(peer, 0).start()

    each_line(1, lambda peer: line_copy(peer, 1).start())

    def advance(c):
        each_line(c - 2, lambda peer: line_copy(peer, c - 2).wait_send())
        each_line(c, lambda peer: line_copy(peer, c).start())

    mine = pltpu.make_async_copy(weight_ref, whole_ref.at[chan], own_sem.at[0])
    mine.start()
    to_twin = remote(weight_ref, whole_ref.at[chan], pair_send.at[0], pair_recv.at[0], (y, z, xlo, twin))
    to_twin.start()

    for copy in caps:
        copy.wait()

    @pl.when(me != 0)
    def _():
        line_copy(0, 0).start()

    own = pltpu.make_async_copy(
        rows_ref.at[pl.ds(me * ROWS, SPAN)], got_ref.at[me], own_sem.at[1]
    )
    own.start()
    for copy in loads:
        copy.wait()

    def one_filter(k, carry):
        for e in range(NNZ):
            tall = jnp.concatenate(
                [basis_ref[e, k], jnp.zeros((128 - 65, 128), jnp.float32)], axis=0
            )
            tmp_ref[e] = tall.T
        for e in range(NNZ):
            taps = tmp_ref[e, pl.ds(pl.multiple_of(me * ROWS, ROWS), ROWS), :]
            filt_ref[pl.ds(e * 16 + k, ROWS, stride=TAPS), :] = taps
        return carry

    lax.fori_loop(0, K, one_filter, 0)
    away = jnp.abs(lax.broadcasted_iota(jnp.int32, (16, 128), 1) - 32)

    def scale(row, carry):
        for e in range(NNZ):
            from_row = src_ref[e, me * ROWS + row]
            quad = quad_ref[jnp.where(from_row < POLE, POLE - 1 - from_row, from_row - POLE)]
            reach = reach_ref[e, me * ROWS + row]
            at = pl.ds(pl.multiple_of(row * TAPS + e * 16, 16), 16)
            kept = jnp.where(away <= reach, filt_ref[at, :] * quad, 0.0)
            filt_ref[at, :] = kept.astype(jnp.bfloat16).astype(jnp.float32)
        return carry

    lax.fori_loop(0, ROWS, scale, 0)

    def fan_z(target):
        return remote(
            whole_ref.at[other, :, piece], whole_ref.at[other, :, piece],
            fan_z_send.at[target], fan_z_recv.at[z], (y, target, xlo, chan),
        )

    @pl.when(owned < K)
    def _():
        across.wait()
        for d in range(1, 4):
            fan_z(lax.rem(z + d, 4)).start()

    advance(2)

    def fan_y(j, target):
        at = whole_ref.at[other, :, part_spot(y + 4 * j)]
        return remote(at, at, fan_y_send.at[j, target], fan_y_recv.at[y, j], (target, z, xlo, chan))

    def fan_y_from(start, j):
        at = whole_ref.at[other, :, start * C + 4 * j * C : start * C + 4 * j * C + C]
        return remote(at, at, fan_y_send.at[j, start], fan_y_recv.at[start, j], (start, z, xlo, chan))

    def each_piece(act):
        for j in range(3):
            if j < 2:
                act(j)
            else:
                pl.when(y == 0)(functools.partial(act, j))

    def pass_on(j):
        at = whole_ref.at[other, :, part_spot(y + 4 * j)]

        @pl.when(z != j)
        def _():
            remote(at, at, fan_z_send.at[0], fan_z_recv.at[j], (y, j, xlo, chan)).wait_recv()

        for d in range(1, 4):
            fan_y(j, lax.rem(y + d, 4)).start()

    each_piece(pass_on)
    advance(3)

    def one_table(b, carry):
        at = pl.multiple_of(b * 96, 96)
        part = u_ref[pl.ds(b, 1), :] * p_ref[...] + v_ref[pl.ds(b, 1), :] * q_ref[...]
        table_ref[pl.ds(at, 96), :] = part.astype(jnp.bfloat16)
        return carry

    lax.fori_loop(0, PLANE, one_table, 0)


    def halo_copy(side, c):
        target = lax.rem(yz + PLANE - 1 + 2 * side, PLANE)
        return remote(
            edge_ref.at[side, pl.ds(4 * c, 4)], halo_ref.at[side, pl.ds(4 * c, 4)],
            halo_send.at[side, c], halo_recv.at[side, c], at_plane(target),
        )

    def joined(first, u):
        return jnp.concatenate(
            [got_ref[first + q, u].astype(jnp.float32)[:, :OWN] for q in range(4)], axis=1
        )

    def arrive(c):
        for d in range(1, LINE):
            slot = lax.rem(me + LINE - d, LINE)
            remote(
                rows_ref.at[pl.ds(0, 4)], got_ref.at[slot, pl.ds(4 * c, 4)],
                line_send.at[slot, c], line_recv.at[slot, c], at_line(slot),
            ).wait_recv()

        def one(i, carry):
            u = 4 * c + i
            left, right = joined(0, u), joined(4, u)
            edge_ref[0, u] = left[:32].astype(jnp.bfloat16)
            edge_ref[1, u] = right[16:].astype(jnp.bfloat16)
            flat_ref[u, 32:77, :] = left[:SLAB]
            flat_ref[u, 77:122, :] = right[3:]
            return carry

        lax.fori_loop(0, 4, one, 0)
        for side in range(2):
            halo_copy(side, c).start()

    def finish(c):
        for side in range(2):
            halo_copy(side, c).wait_recv()

        def one(i, carry):
            u = 4 * c + i
            flat_ref[u, 0:32, :] = halo_ref[1, u].astype(jnp.float32)
            flat_ref[u, 122:154, :] = halo_ref[0, u].astype(jnp.float32)
            flat_ref[u, 154:EXT, :] = jnp.zeros((EXT - 154, C), jnp.float32)
            x_ref[u] = flat_ref[u].astype(jnp.bfloat16)
            return carry

        lax.fori_loop(0, 4, one, 0)

    odd = lax.rem(me, 2) == 1
    twin_copy = remote(
        x_ref.at[pl.ds(0, 8)], land_ref, pair_send.at[2], pair_recv.at[2], (y, z, xlo, twin)
    )

    def late(c):
        @pl.when(odd)
        def _():
            finish(c)

        @pl.when(jnp.logical_not(odd) & (c == 4))
        def _():
            twin_copy.wait_recv()

        @pl.when(jnp.logical_not(odd))
        def _():
            def one(i, carry):
                x_ref[4 * c + i] = land_ref[4 * c - 16 + i]
                return carry

            lax.fori_loop(0, 4, one, 0)

    far_copy = remote(
        whole_ref.at[other], whole_ref.at[other], pair_send.at[1], pair_recv.at[1], (y, z, xlo, twin)
    )
    own.wait()
    arrive(0)
    advance(4)
    arrive(1)
    arrive(2)
    advance(5)
    for start in range(4):
        for j in range(3 if start == 0 else 2):

            @pl.when(y != start)
            def _():
                fan_y_from(start, j).wait_recv()

    far_copy.start()
    for c in range(3):
        finish(c)

    @pl.when(odd)
    def _():
        twin_copy.start()

    lane = lax.broadcasted_iota(jnp.int32, (TILE, 128), 1)

    def build(row, band_ref):
        for k in range(K):
            turned = []
            for e in range(NNZ):
                taps = filt_ref[pl.ds(row * TAPS + e * 16 + k, 1), :]
                spread = jnp.broadcast_to(taps, (TILE, 128))
                turned.append(pltpu.roll(spread, 96 * e % 128, 1, stride=1, stride_axis=0))
            tiles = [
                jnp.where(lane < 96, turned[0], turned[1]),
                jnp.where(lane < 64, turned[1], turned[2]),
                jnp.where(lane < 32, turned[2], turned[3]),
                turned[4],
            ]
            for t in range(4):
                band_ref[k * TILE : (k + 1) * TILE, t * 128 : (t + 1) * 128] = tiles[t].astype(jnp.bfloat16)

    def convolve(row, band_ref):
        sources = [jnp.clip(src_ref[e, me * ROWS + row] - me * ROWS, 0, SPAN - 1) for e in range(NNZ)]
        windows = []
        for b in range(3):
            pieces = [x_ref[u, b * TILE : b * TILE + 96, :] for u in sources]
            windows.append(jnp.concatenate(pieces + [x_ref[sources[0], 0:32, :]], axis=0))
        total = jnp.dot(
            band_ref[...], jnp.concatenate(windows, axis=1), preferred_element_type=jnp.float32
        )
        rounded = total.astype(jnp.bfloat16)
        for b in range(3):
            at = pl.multiple_of(lax.rem(row, 4) * 96 + b * TILE, TILE)
            for k in range(K):
                filtered_ref[pl.ds(at, TILE), k * C : (k + 1) * C] = rounded[
                    k * TILE : (k + 1) * TILE, b * C : (b + 1) * C
                ]

    ty, tz = me // 2, lax.rem(me, 2) * 2

    def to_self(s, o):
        return (ty == y) & (tz + s // 2 == z) & (lax.rem(s, 2) == xlo) & (chan == o)

    def send_copy(s, o):
        return remote(
            sent_ref.at[s, o], all_ref.at[yz], send_sem.at[s, o], recv_sem.at[yz],
            (ty, tz + s // 2, lax.rem(s, 2), o),
        )

    def own_copy(s, o):
        return pltpu.make_async_copy(sent_ref.at[s, o], all_ref.at[yz], own_sem.at[2])

    build(0, even_ref)

    def pair(p, carry):
        c = p // 2

        @pl.when(p == 2)
        def _():
            finish(3)

        @pl.when((lax.rem(p, 2) == 0) & (p > 2))
        def _():
            late(c + 2)

        convolve(2 * p, even_ref)
        build(2 * p + 1, odd_ref)
        convolve(2 * p + 1, odd_ref)
        build(jnp.minimum(2 * p + 2, ROWS - 1), even_ref)

        @pl.when((p == 0) | ((p < 3) & odd))
        def _():
            arrive(p + 3)

        @pl.when(p == 1)
        def _():
            far_copy.wait()
            to_twin.wait()
            pl.semaphore_wait(ready_sem, LINE - 1)
            mine.wait()

        @pl.when(lax.rem(p, 2) == 1)
        def _():
            acc = lax.dot_general(
                filtered_ref[...],
                whole_ref[...].reshape(C, K * C),
                (((1,), (1,)), ((), ())),
                preferred_element_type=jnp.float32,
            )
            for o in range(4):
                joint = jnp.concatenate(
                    [acc[i * 96 : (i + 1) * 96, o * OWN : (o + 1) * OWN] for i in range(4)], axis=1
                )
                sent_ref[c, o] = joint.astype(jnp.bfloat16)
            for o in range(4):

                @pl.when(to_self(c, o))
                def _():
                    own_copy(c, o).start()

                @pl.when(jnp.logical_not(to_self(c, o)))
                def _():
                    send_copy(c, o).start()

        return carry

    lax.fori_loop(0, 8, pair, 0)

    for s in range(4):
        for o in range(4):

            @pl.when(to_self(s, o))
            def _():
                own_copy(s, o).wait()

            @pl.when(jnp.logical_not(to_self(s, o)))
            def _():
                send_copy(s, o).wait_send()

    for c in range(PARTS):

        def edges_left(c=c):
            for side in range(2):
                halo_copy(side, c).wait_send()

        if c < 4:
            edges_left()
        else:
            pl.when(odd)(edges_left)
        if c >= 4:
            each_line(c, lambda peer: line_copy(peer, c).wait_send())

    @pl.when(odd)
    def _():
        twin_copy.wait_send()

    @pl.when(owned < K)
    def _():
        for d in range(1, 4):
            fan_z(lax.rem(z + d, 4)).wait_send()

    def left(j):
        for d in range(1, 4):
            fan_y(j, lax.rem(y + d, 4)).wait_send()

    each_piece(left)

    for b in range(PLANE):

        @pl.when(jnp.logical_not(jnp.logical_and(b == yz, source == me)))
        def _():
            remote(
                sent_ref.at[0, 0], all_ref.at[b], send_sem.at[0, 0], recv_sem.at[b], (b // 4, b % 4, xlo, chan)
            ).wait_recv()

    result = lax.dot_general(
        all_ref[...].reshape(PLANE * 96, C),
        table_ref[...],
        (((0,), (0,)), ((), ())),
        preferred_element_type=jnp.float32,
    )
    for t in range(12):
        result_ref[t * C : (t + 1) * C, :] = result[:, 128 * t : 128 * (t + 1)]

    def out_copy(g):
        at = pl.ds(45 * g, 45)
        return pltpu.make_async_copy(stage_ref.at[at], out_ref.at[at], out_sem.at[g])

    def store(g, carry):
        pieces = []
        for j in range(4):
            tiles = [result_ref[pl.ds(t * C + 4 * g + j, 4, stride=OWN), :] for t in range(12)]
            pieces += tiles[:11] + [tiles[11][:, :32]]
        four = jnp.concatenate(pieces, axis=1)
        for t in range(45):
            stage_ref[45 * g + t] = four[:, 128 * t : 128 * (t + 1)]
        out_copy(g).start()
        return carry

    lax.fori_loop(0, OWN // 4, store, 0)
    for g in range(OWN // 4):
        out_copy(g).wait()


def layer(src, reach, quads, fields, weight, basis, tables):
    vmem = pl.BlockSpec(memory_space=pltpu.VMEM)
    smem = pl.BlockSpec(memory_space=pltpu.SMEM)
    dma = pltpu.SemaphoreType.DMA
    wide = 128 + 2 * POLE
    bf16 = jnp.bfloat16
    return pl.pallas_call(
        layer_kernel,
        out_shape=jax.ShapeDtypeStruct((OWN * 2 * MODES // 128, 4, 128), jnp.float32),
        in_specs=[smem] * 3 + [vmem] * 2 + [pl.BlockSpec(memory_space=pl.ANY)] * 5,
        out_specs=pl.BlockSpec(memory_space=pl.ANY),
        scratch_shapes=[
            *[pltpu.VMEM(a.shape, a.dtype) for a in (basis, *tables)],
            dma((5,)),
            pltpu.VMEM((OWN * PAD, 128), jnp.float32),
            pltpu.VMEM((wide * PAD, 128), jnp.float32),
            pltpu.VMEM((wide, PAD, 128), bf16),
            pltpu.VMEM((NNZ, 128, 128), jnp.float32),
            pltpu.VMEM((LINE, SPAN, PAD, 128), bf16),
            pltpu.VMEM((2, SPAN, 32, C), bf16),
            pltpu.VMEM((2, SPAN, 32, C), bf16),
            pltpu.VMEM((8, EXT, C), bf16),
            pltpu.VMEM((4, OWN, K * C), bf16),
            pltpu.VMEM((ROWS * TAPS, 128), jnp.float32),
            pltpu.VMEM((SPAN, EXT, C), jnp.float32),
            pltpu.VMEM((SPAN, EXT, C), bf16),
            pltpu.VMEM((K * TILE, 512), bf16),
            pltpu.VMEM((K * TILE, 512), bf16),
            pltpu.VMEM((4 * 96, K * C), bf16),
            pltpu.VMEM((4, 4, 96, C), bf16),
            pltpu.VMEM((PLANE, 96, C), bf16),
            pltpu.VMEM((PLANE * 96, 1536), bf16),
            pltpu.VMEM((12 * C, 128), jnp.float32),
            dma((LINE, PARTS)), dma((LINE, PARTS)), dma((POLE,)), dma((POLE,)), dma((2, PARTS)), dma((2, PARTS)),
            dma, dma, dma((3,)), dma((3,)), dma((4,)), dma((4,)), dma((3, 4)), dma((4, 3)), dma((3,)),
            dma((4, 4)), dma((PLANE,)), pltpu.SemaphoreType.REGULAR,
            pltpu.VMEM((OWN * 2 * MODES // 128, 4, 128), jnp.float32), dma((OWN // 4,)),
        ],
        compiler_params=pltpu.CompilerParams(
            collective_id=0, has_side_effects=True, vmem_limit_bytes=60 << 20
        ),
    )(src, reach, quads, fields, weight, basis, *tables)


def dft_parts():
    modes = np.arange(MODES)
    high = 2 * math.pi * ((np.arange(PLANE)[:, None] * WIDTH * modes[None]) % NLON) / NLON
    low = 2 * math.pi * ((np.arange(96)[:, None] * modes[None]) % NLON) / NLON
    factor = 1 / math.sqrt(NLON)
    inside = (np.arange(96) < WIDTH)[:, None]
    ca, sa = np.cos(high) * factor, np.sin(high) * factor
    cb, sb = np.cos(low) * inside, np.sin(low) * inside
    side = lambda a, b: jnp.asarray(np.concatenate([a, b, 0 * a[:, :96]], axis=1), jnp.float32)
    return side(cb, cb), side(sb, sb), side(ca, -sa), side(-sa, -ca)


def shards(fields, mix_weight, basis_values, source_rows, lon_reach, quad_weights):
    out = layer(
        source_rows.T, lon_reach.T, quad_weights, fields, mix_weight, basis_values, dft_parts()
    )
    return out.transpose(1, 0, 2).reshape(4, OWN * 2 * MODES)


def solution(mesh):
    fine = Mesh(mesh.devices.reshape(4, 4, 2, 4), ("y", "z", "xlo", "chan"))
    lon = ("y", "z", "xlo")
    placed = (P(lon, "chan"), P("chan", None), P(), P(), P(), P())
    return jax.shard_map(
        shards, mesh=fine, in_specs=placed, out_specs=P(lon, "chan"), check_vma=False
    )
```

```python
import functools
import math

import jax
import jax.numpy as jnp
import numpy as np
from jax import lax
from jax.experimental import pallas as pl
from jax.experimental.pallas import tpu as pltpu
from jax.sharding import Mesh, PartitionSpec as P

C = 384
MODES = 720
NLON = 1440
K = 9
NNZ = 5
POLE = 4
LINE = 8
PLANE = 16
ROWS = 16
SPAN = 24
SLAB = 45
OWN = 96
PAD = 48
WIDTH = 90
TILE = 32
EXT = 160
TAPS = 80
PARTS = 6
MESH = pl.DeviceIdType.MESH


def place():
    y, z = lax.axis_index("y"), lax.axis_index("z")
    xlo, chan = lax.axis_index("xlo"), lax.axis_index("chan")
    return y, z, xlo, chan, y * 4 + z, xlo * 4 + chan


def remote(src, dst, send, recv, where):
    return pltpu.make_async_remote_copy(
        src_ref=src, dst_ref=dst, send_sem=send, recv_sem=recv, device_id=where, device_id_type=MESH
    )


def layer_kernel(
    src_ref, reach_ref, quad_ref, fields_ref, weight_ref, basis_in, p_in, q_in, u_in, v_in,
    out_ref,
    basis_ref, p_ref, q_ref, u_ref, v_ref, load_sem,
    tall_ref, wide_ref, rows_ref, tmp_ref, got_ref, edge_ref, halo_ref, land_ref, whole_ref, filt_ref, flat_ref, x_ref,
    even_ref, odd_ref, filtered_ref, sent_ref, all_ref, table_ref, result_ref,
    line_send, line_recv, cap_send, cap_recv, halo_send, halo_recv,
    part_send, part_recv, pair_send, pair_recv, fan_z_send, fan_z_recv, fan_y_send, fan_y_recv, own_sem,
    send_sem, recv_sem, ready_sem, stage_ref, out_sem,
):
    y, z, xlo, chan, yz, me = place()
    at_line = lambda p: (y, z, p // 4, lax.rem(p, 4))
    at_plane = lambda p: (p // 4, lax.rem(p, 4), xlo, chan)
    source = 2 * y + z // 2
    barrier = pltpu.get_barrier_semaphore()

    def signal(where):
        pl.semaphore_signal(barrier, inc=1, device_id=where, device_id_type=MESH)

    for d in range(1, LINE):
        signal(at_line(lax.rem(me + d, LINE)))
    for d in range(1, PLANE):
        signal(at_plane(lax.rem(yz + d, PLANE)))
    loads = [
        pltpu.make_async_copy(a, b, load_sem.at[i])
        for i, (a, b) in enumerate(
            [(basis_in, basis_ref), (p_in, p_ref), (q_in, q_ref), (u_in, u_ref), (v_in, v_ref)]
        )
    ]
    for copy in loads:
        copy.start()

    for c in range(OWN):
        tall_ref[c * PAD : c * PAD + SLAB, :] = fields_ref[:, c * 128 : (c + 1) * 128].astype(jnp.float32)
    shift = POLE * PAD + 3 * xlo
    zeros = jnp.zeros((128 - OWN, 128), jnp.float32)
    for l in range(SLAB):
        turned = jnp.concatenate([tall_ref[pl.ds(l, OWN, stride=PAD), :], zeros], axis=0).T
        wide_ref[pl.ds(shift + l, 128, stride=PAD), :] = turned

    def narrow(row, carry):
        at = pl.multiple_of(row * PAD, PAD)
        rows_ref[row] = wide_ref[pl.ds(at, PAD), :].astype(jnp.bfloat16)
        return carry

    lax.fori_loop(POLE, POLE + 128, narrow, 0, unroll=4)
    rows_ref[POLE + 128 :] = jnp.zeros((POLE, PAD, 128), jnp.bfloat16)

    pl.semaphore_wait(barrier, LINE + PLANE - 2)
    for d in range(1, LINE):
        pl.semaphore_signal(
            ready_sem, inc=1, device_id=at_line(lax.rem(me + d, LINE)), device_id_type=MESH
        )

    caps = [
        remote(
            rows_ref.at[POLE + g], rows_ref.at[POLE - 1 - g], cap_send.at[g], cap_recv.at[g],
            (lax.rem(y + 2, 4), z, xlo, chan),
        )
        for g in range(POLE)
    ]
    for copy in caps:
        copy.start()

    other = lax.rem(chan + 2, 4)
    twin = chan + 1 - 2 * lax.rem(chan, 2)
    part_spot = lambda p: pl.ds(pl.multiple_of(p * C, 128), C)
    owned = y + 4 * z
    piece = part_spot(lax.rem(owned, K))
    across = remote(
        weight_ref.at[:, piece], whole_ref.at[chan, :, piece], part_send, part_recv, (y, z, 1 - xlo, other)
    )

    @pl.when(owned < K)
    def _():
        across.start()

    def line_copy(peer, c):
        return remote(
            rows_ref.at[pl.ds(peer * ROWS + 4 * c, 4)], got_ref.at[me, pl.ds(4 * c, 4)],
            line_send.at[peer, c], line_recv.at[me, c], at_line(peer),
        )

    def takes(peer, c):
        return lax.rem(peer, 2) * 2 + 4 > c

    def each_line(c, act):
        for d in range(1, LINE):
            peer = lax.rem(me + d, LINE)
            if isinstance(c, int) and c < 4:
                act(peer)
            else:
                pl.when(takes(peer, c))(functools.partial(act, peer))

    for d in range(1, LINE):
        peer = lax.rem(me + d, LINE)

        @pl.when(peer != 0)
        def _():
            line_copy(peer, 0).start()

    each_line(1, lambda peer: line_copy(peer, 1).start())

    def advance(c):
        each_line(c - 2, lambda peer: line_copy(peer, c - 2).wait_send())
        each_line(c, lambda peer: line_copy(peer, c).start())

    mine = pltpu.make_async_copy(weight_ref, whole_ref.at[chan], own_sem.at[0])
    mine.start()
    to_twin = remote(weight_ref, whole_ref.at[chan], pair_send.at[0], pair_recv.at[0], (y, z, xlo, twin))
    to_twin.start()

    for copy in caps:
        copy.wait()

    @pl.when(me != 0)
    def _():
        line_copy(0, 0).start()

    own = pltpu.make_async_copy(
        rows_ref.at[pl.ds(me * ROWS, SPAN)], got_ref.at[me], own_sem.at[1]
    )
    own.start()
    for copy in loads:
        copy.wait()

    def one_filter(k, carry):
        for e in range(NNZ):
            tall = jnp.concatenate(
                [basis_ref[e, k], jnp.zeros((128 - 65, 128), jnp.float32)], axis=0
            )
            tmp_ref[e] = tall.T
        for e in range(NNZ):
            taps = tmp_ref[e, pl.ds(pl.multiple_of(me * ROWS, ROWS), ROWS), :]
            filt_ref[pl.ds(e * 16 + k, ROWS, stride=TAPS), :] = taps
        return carry

    lax.fori_loop(0, K, one_filter, 0)
    away = jnp.abs(lax.broadcasted_iota(jnp.int32, (16, 128), 1) - 32)

    def scale(row, carry):
        for e in range(NNZ):
            from_row = src_ref[e, me * ROWS + row]
            quad = quad_ref[jnp.where(from_row < POLE, POLE - 1 - from_row, from_row - POLE)]
            reach = reach_ref[e, me * ROWS + row]
            at = pl.ds(pl.multiple_of(row * TAPS + e * 16, 16), 16)
            kept = jnp.where(away <= reach, filt_ref[at, :] * quad, 0.0)
            filt_ref[at, :] = kept.astype(jnp.bfloat16).astype(jnp.float32)
        return carry

    lax.fori_loop(0, ROWS, scale, 0)

    def fan_z(target):
        return remote(
            whole_ref.at[other, :, piece], whole_ref.at[other, :, piece],
            fan_z_send.at[target], fan_z_recv.at[z], (y, target, xlo, chan),
        )

    @pl.when(owned < K)
    def _():
        across.wait()
        for d in range(1, 4):
            fan_z(lax.rem(z + d, 4)).start()

    advance(2)

    def fan_y(j, target):
        at = whole_ref.at[other, :, part_spot(y + 4 * j)]
        return remote(at, at, fan_y_send.at[j, target], fan_y_recv.at[y, j], (target, z, xlo, chan))

    def fan_y_from(start, j):
        at = whole_ref.at[other, :, start * C + 4 * j * C : start * C + 4 * j * C + C]
        return remote(at, at, fan_y_send.at[j, start], fan_y_recv.at[start, j], (start, z, xlo, chan))

    def each_piece(act):
        for j in range(3):
            if j < 2:
                act(j)
            else:
                pl.when(y == 0)(functools.partial(act, j))

    def pass_on(j):
        at = whole_ref.at[other, :, part_spot(y + 4 * j)]

        @pl.when(z != j)
        def _():
            remote(at, at, fan_z_send.at[0], fan_z_recv.at[j], (y, j, xlo, chan)).wait_recv()

        for d in range(1, 4):
            fan_y(j, lax.rem(y + d, 4)).start()

    each_piece(pass_on)
    advance(3)

    def one_table(b, carry):
        at = pl.multiple_of(b * 96, 96)
        part = u_ref[pl.ds(b, 1), :] * p_ref[...] + v_ref[pl.ds(b, 1), :] * q_ref[...]
        table_ref[pl.ds(at, 96), :] = part.astype(jnp.bfloat16)
        return carry

    lax.fori_loop(0, PLANE, one_table, 0)


    def halo_copy(side, c):
        target = lax.rem(yz + PLANE - 1 + 2 * side, PLANE)
        return remote(
            edge_ref.at[side, pl.ds(4 * c, 4)], halo_ref.at[side, pl.ds(4 * c, 4)],
            halo_send.at[side, c], halo_recv.at[side, c], at_plane(target),
        )

    def joined(first, u):
        return jnp.concatenate(
            [got_ref[first + q, u].astype(jnp.float32)[:, :OWN] for q in range(4)], axis=1
        )

    def arrive(c):
        for d in range(1, LINE):
            slot = lax.rem(me + LINE - d, LINE)
            remote(
                rows_ref.at[pl.ds(0, 4)], got_ref.at[slot, pl.ds(4 * c, 4)],
                line_send.at[slot, c], line_recv.at[slot, c], at_line(slot),
            ).wait_recv()

        def one(i, carry):
            u = 4 * c + i
            left, right = joined(0, u), joined(4, u)
            edge_ref[0, u] = left[:32].astype(jnp.bfloat16)
            edge_ref[1, u] = right[16:].astype(jnp.bfloat16)
            flat_ref[u, 32:77, :] = left[:SLAB]
            flat_ref[u, 77:122, :] = right[3:]
            return carry

        lax.fori_loop(0, 4, one, 0)
        for side in range(2):
            halo_copy(side, c).start()

    def finish(c):
        for side in range(2):
            halo_copy(side, c).wait_recv()

        def one(i, carry):
            u = 4 * c + i
            flat_ref[u, 0:32, :] = halo_ref[1, u].astype(jnp.float32)
            flat_ref[u, 122:154, :] = halo_ref[0, u].astype(jnp.float32)
            flat_ref[u, 154:EXT, :] = jnp.zeros((EXT - 154, C), jnp.float32)
            x_ref[u] = flat_ref[u].astype(jnp.bfloat16)
            return carry

        lax.fori_loop(0, 4, one, 0)

    twin_copy = remote(
        x_ref.at[pl.ds(0, 8)], land_ref, pair_send.at[2], pair_recv.at[2], (y, z, xlo, twin)
    )

    def late(c):
        @pl.when(odd)
        def _():
            finish(c)

        @pl.when(jnp.logical_not(odd) & (c == 4))
        def _():
            twin_copy.wait_recv()

        @pl.when(jnp.logical_not(odd))
        def _():
            def one(i, carry):
                x_ref[4 * c + i] = land_ref[4 * c - 16 + i]
                return carry

            lax.fori_loop(0, 4, one, 0)

    far_copy = remote(
        whole_ref.at[other], whole_ref.at[other], pair_send.at[1], pair_recv.at[1], (y, z, xlo, twin)
    )
    odd = lax.rem(me, 2) == 1
    own.wait()
    arrive(0)
    advance(4)
    arrive(1)
    arrive(2)
    advance(5)
    arrive(3)

    @pl.when(odd)
    def _():
        arrive(4)

    for start in range(4):
        for j in range(3 if start == 0 else 2):

            @pl.when(y != start)
            def _():
                fan_y_from(start, j).wait_recv()

    far_copy.start()
    for c in range(3):
        finish(c)

    @pl.when(odd)
    def _():
        twin_copy.start()

    lane = lax.broadcasted_iota(jnp.int32, (TILE, 128), 1)

    def build(row, band_ref):
        for k in range(K):
            turned = []
            for e in range(NNZ):
                taps = filt_ref[pl.ds(row * TAPS + e * 16 + k, 1), :]
                spread = jnp.broadcast_to(taps, (TILE, 128))
                turned.append(pltpu.roll(spread, 96 * e % 128, 1, stride=1, stride_axis=0))
            tiles = [
                jnp.where(lane < 96, turned[0], turned[1]),
                jnp.where(lane < 64, turned[1], turned[2]),
                jnp.where(lane < 32, turned[2], turned[3]),
                turned[4],
            ]
            for t in range(4):
                band_ref[k * TILE : (k + 1) * TILE, t * 128 : (t + 1) * 128] = tiles[t].astype(jnp.bfloat16)

    def convolve(row, band_ref):
        sources = [jnp.clip(src_ref[e, me * ROWS + row] - me * ROWS, 0, SPAN - 1) for e in range(NNZ)]
        windows = []
        for b in range(3):
            pieces = [x_ref[u, b * TILE : b * TILE + 96, :] for u in sources]
            windows.append(jnp.concatenate(pieces + [x_ref[sources[0], 0:32, :]], axis=0))
        total = jnp.dot(
            band_ref[...], jnp.concatenate(windows, axis=1), preferred_element_type=jnp.float32
        )
        rounded = total.astype(jnp.bfloat16)
        for b in range(3):
            at = pl.multiple_of(lax.rem(row, 4) * 96 + b * TILE, TILE)
            for k in range(K):
                filtered_ref[pl.ds(at, TILE), k * C : (k + 1) * C] = rounded[
                    k * TILE : (k + 1) * TILE, b * C : (b + 1) * C
                ]

    ty, tz = me // 2, lax.rem(me, 2) * 2

    def to_self(s, o):
        return (ty == y) & (tz + s // 2 == z) & (lax.rem(s, 2) == xlo) & (chan == o)

    def send_copy(s, o):
        return remote(
            sent_ref.at[s, o], all_ref.at[yz], send_sem.at[s, o], recv_sem.at[yz],
            (ty, tz + s // 2, lax.rem(s, 2), o),
        )

    def own_copy(s, o):
        return pltpu.make_async_copy(sent_ref.at[s, o], all_ref.at[yz], own_sem.at[2])

    build(0, even_ref)

    def pair(p, carry):
        c = p // 2

        @pl.when(p == 2)
        def _():
            finish(3)

        @pl.when((lax.rem(p, 2) == 0) & (p > 2))
        def _():
            late(c + 2)

        convolve(2 * p, even_ref)
        build(2 * p + 1, odd_ref)
        convolve(2 * p + 1, odd_ref)
        build(jnp.minimum(2 * p + 2, ROWS - 1), even_ref)

        @pl.when((p == 0) & odd)
        def _():
            arrive(5)

        @pl.when(p == 1)
        def _():
            far_copy.wait()
            to_twin.wait()
            pl.semaphore_wait(ready_sem, LINE - 1)
            mine.wait()

        @pl.when(lax.rem(p, 2) == 1)
        def _():
            acc = lax.dot_general(
                filtered_ref[...],
                whole_ref[...].reshape(C, K * C),
                (((1,), (1,)), ((), ())),
                preferred_element_type=jnp.float32,
            )
            for o in range(4):
                joint = jnp.concatenate(
                    [acc[i * 96 : (i + 1) * 96, o * OWN : (o + 1) * OWN] for i in range(4)], axis=1
                )
                sent_ref[c, o] = joint.astype(jnp.bfloat16)
            for o in range(4):

                @pl.when(to_self(c, o))
                def _():
                    own_copy(c, o).start()

                @pl.when(jnp.logical_not(to_self(c, o)))
                def _():
                    send_copy(c, o).start()

        return carry

    lax.fori_loop(0, 8, pair, 0)

    for s in range(4):
        for o in range(4):

            @pl.when(to_self(s, o))
            def _():
                own_copy(s, o).wait()

            @pl.when(jnp.logical_not(to_self(s, o)))
            def _():
                send_copy(s, o).wait_send()

    for c in range(PARTS):

        def edges_left(c=c):
            for side in range(2):
                halo_copy(side, c).wait_send()

        if c < 4:
            edges_left()
        else:
            pl.when(odd)(edges_left)
        if c >= 4:
            each_line(c, lambda peer: line_copy(peer, c).wait_send())

    @pl.when(odd)
    def _():
        twin_copy.wait_send()

    @pl.when(owned < K)
    def _():
        for d in range(1, 4):
            fan_z(lax.rem(z + d, 4)).wait_send()

    def left(j):
        for d in range(1, 4):
            fan_y(j, lax.rem(y + d, 4)).wait_send()

    each_piece(left)

    for b in range(PLANE):

        @pl.when(jnp.logical_not(jnp.logical_and(b == yz, source == me)))
        def _():
            remote(
                sent_ref.at[0, 0], all_ref.at[b], send_sem.at[0, 0], recv_sem.at[b], (b // 4, b % 4, xlo, chan)
            ).wait_recv()

    result = lax.dot_general(
        all_ref[...].reshape(PLANE * 96, C),
        table_ref[...],
        (((0,), (0,)), ((), ())),
        preferred_element_type=jnp.float32,
    )
    for t in range(12):
        result_ref[t * C : (t + 1) * C, :] = result[:, 128 * t : 128 * (t + 1)]

    def out_copy(g):
        at = pl.ds(45 * g, 45)
        return pltpu.make_async_copy(stage_ref.at[at], out_ref.at[at], out_sem.at[g])

    def store(g, carry):
        tiles = []
        for j in range(8):
            tiles.append([result_ref[pl.ds(t * C + 8 * g + j, 4, stride=OWN), :] for t in range(12)])
        flat = []
        for half in range(2):
            pieces = []
            for j in range(4):
                pieces += tiles[4 * half + j][:11] + [tiles[4 * half + j][11][:, :32]]
            four = jnp.concatenate(pieces, axis=1)
            flat += [four[:, 128 * t : 128 * (t + 1)] for t in range(45)]
        for t in range(45):
            stage_ref[45 * g + t] = jnp.concatenate(flat[2 * t : 2 * t + 2], axis=0)
        out_copy(g).start()
        return carry

    lax.fori_loop(0, OWN // 8, store, 0)
    for g in range(OWN // 8):
        out_copy(g).wait()


def layer(src, reach, quads, fields, weight, basis, tables):
    vmem = pl.BlockSpec(memory_space=pltpu.VMEM)
    smem = pl.BlockSpec(memory_space=pltpu.SMEM)
    dma = pltpu.SemaphoreType.DMA
    wide = 128 + 2 * POLE
    bf16 = jnp.bfloat16
    return pl.pallas_call(
        layer_kernel,
        out_shape=jax.ShapeDtypeStruct((OWN * MODES // 128, 8, 128), jnp.float32),
        in_specs=[smem] * 3 + [vmem] * 2 + [pl.BlockSpec(memory_space=pl.ANY)] * 5,
        out_specs=pl.BlockSpec(memory_space=pl.ANY),
        scratch_shapes=[
            *[pltpu.VMEM(a.shape, a.dtype) for a in (basis, *tables)],
            dma((5,)),
            pltpu.VMEM((OWN * PAD, 128), jnp.float32),
            pltpu.VMEM((wide * PAD, 128), jnp.float32),
            pltpu.VMEM((wide, PAD, 128), bf16),
            pltpu.VMEM((NNZ, 128, 128), jnp.float32),
            pltpu.VMEM((LINE, SPAN, PAD, 128), bf16),
            pltpu.VMEM((2, SPAN, 32, C), bf16),
            pltpu.VMEM((2, SPAN, 32, C), bf16),
            pltpu.VMEM((8, EXT, C), bf16),
            pltpu.VMEM((4, OWN, K * C), bf16),
            pltpu.VMEM((ROWS * TAPS, 128), jnp.float32),
            pltpu.VMEM((SPAN, EXT, C), jnp.float32),
            pltpu.VMEM((SPAN, EXT, C), bf16),
            pltpu.VMEM((K * TILE, 512), bf16),
            pltpu.VMEM((K * TILE, 512), bf16),
            pltpu.VMEM((4 * 96, K * C), bf16),
            pltpu.VMEM((4, 4, 96, C), bf16),
            pltpu.VMEM((PLANE, 96, C), bf16),
            pltpu.VMEM((PLANE * 96, 1536), bf16),
            pltpu.VMEM((12 * C, 128), jnp.float32),
            dma((LINE, PARTS)), dma((LINE, PARTS)), dma((POLE,)), dma((POLE,)), dma((2, PARTS)), dma((2, PARTS)),
            dma, dma, dma((3,)), dma((3,)), dma((4,)), dma((4,)), dma((3, 4)), dma((4, 3)), dma((3,)),
            dma((4, 4)), dma((PLANE,)), pltpu.SemaphoreType.REGULAR,
            pltpu.VMEM((OWN * MODES // 128, 8, 128), jnp.float32), dma((OWN // 8,)),
        ],
        compiler_params=pltpu.CompilerParams(
            collective_id=0, has_side_effects=True, vmem_limit_bytes=60 << 20
        ),
    )(src, reach, quads, fields, weight, basis, *tables)


def dft_parts():
    modes = np.arange(MODES)
    high = 2 * math.pi * ((np.arange(PLANE)[:, None] * WIDTH * modes[None]) % NLON) / NLON
    low = 2 * math.pi * ((np.arange(96)[:, None] * modes[None]) % NLON) / NLON
    factor = 1 / math.sqrt(NLON)
    inside = (np.arange(96) < WIDTH)[:, None]
    ca, sa = np.cos(high) * factor, np.sin(high) * factor
    cb, sb = np.cos(low) * inside, np.sin(low) * inside
    side = lambda a, b: jnp.asarray(np.concatenate([a, b, 0 * a[:, :96]], axis=1), jnp.float32)
    return side(cb, cb), side(sb, sb), side(ca, -sa), side(-sa, -ca)


def shards(fields, mix_weight, basis_values, source_rows, lon_reach, quad_weights):
    out = layer(
        source_rows.T, lon_reach.T, quad_weights, fields, mix_weight, basis_values, dft_parts()
    )
    out = out.reshape(OWN * 2 * MODES // 128, 4, 128)
    return out.transpose(1, 0, 2).reshape(4, OWN * 2 * MODES)


def solution(mesh):
    fine = Mesh(mesh.devices.reshape(4, 4, 2, 4), ("y", "z", "xlo", "chan"))
    lon = ("y", "z", "xlo")
    placed = (P(lon, "chan"), P("chan", None), P(), P(), P(), P())
    return jax.shard_map(
        shards, mesh=fine, in_specs=placed, out_specs=P(lon, "chan"), check_vma=False
    )
```

```python
import functools
import math

import jax
import jax.numpy as jnp
import numpy as np
from jax import lax
from jax.experimental import pallas as pl
from jax.experimental.pallas import tpu as pltpu
from jax.sharding import Mesh, PartitionSpec as P

C = 384
MODES = 720
NLON = 1440
K = 9
NNZ = 5
POLE = 4
LINE = 8
PLANE = 16
ROWS = 16
SPAN = 24
SLAB = 45
OWN = 96
PAD = 48
WIDTH = 90
TILE = 32
EXT = 160
TAPS = 80
PARTS = 6
MESH = pl.DeviceIdType.MESH


def place():
    y, z = lax.axis_index("y"), lax.axis_index("z")
    xlo, chan = lax.axis_index("xlo"), lax.axis_index("chan")
    return y, z, xlo, chan, y * 4 + z, xlo * 4 + chan


def remote(src, dst, send, recv, where):
    return pltpu.make_async_remote_copy(
        src_ref=src, dst_ref=dst, send_sem=send, recv_sem=recv, device_id=where, device_id_type=MESH
    )


def layer_kernel(
    src_ref, reach_ref, quad_ref, fields_ref, weight_ref, basis_in, p_in, q_in, u_in, v_in,
    out_ref,
    basis_ref, p_ref, q_ref, u_ref, v_ref, load_sem,
    tall_ref, wide_ref, rows_ref, tmp_ref, got_ref, edge_ref, halo_ref, land_ref, whole_ref, filt_ref, flat_ref, x_ref,
    even_ref, odd_ref, filtered_ref, sent_ref, all_ref, table_ref, result_ref,
    line_send, line_recv, cap_send, cap_recv, halo_send, halo_recv,
    part_send, part_recv, pair_send, pair_recv, fan_z_send, fan_z_recv, fan_y_send, fan_y_recv, own_sem,
    send_sem, recv_sem, ready_sem, stage_ref, out_sem,
):
    y, z, xlo, chan, yz, me = place()
    at_line = lambda p: (y, z, p // 4, lax.rem(p, 4))
    at_plane = lambda p: (p // 4, lax.rem(p, 4), xlo, chan)
    source = 2 * y + z // 2
    barrier = pltpu.get_barrier_semaphore()

    def signal(where):
        pl.semaphore_signal(barrier, inc=1, device_id=where, device_id_type=MESH)

    for d in range(1, LINE):
        signal(at_line(lax.rem(me + d, LINE)))
    for d in range(1, PLANE):
        signal(at_plane(lax.rem(yz + d, PLANE)))
    loads = [
        pltpu.make_async_copy(a, b, load_sem.at[i])
        for i, (a, b) in enumerate(
            [(basis_in, basis_ref), (p_in, p_ref), (q_in, q_ref), (u_in, u_ref), (v_in, v_ref)]
        )
    ]
    for copy in loads:
        copy.start()

    for c in range(OWN):
        tall_ref[c * PAD : c * PAD + SLAB, :] = fields_ref[:, c * 128 : (c + 1) * 128].astype(jnp.float32)
    shift = POLE * PAD + 3 * xlo
    zeros = jnp.zeros((128 - OWN, 128), jnp.float32)
    for l in range(SLAB):
        turned = jnp.concatenate([tall_ref[pl.ds(l, OWN, stride=PAD), :], zeros], axis=0).T
        wide_ref[pl.ds(shift + l, 128, stride=PAD), :] = turned

    def narrow(row, carry):
        at = pl.multiple_of(row * PAD, PAD)
        rows_ref[row] = wide_ref[pl.ds(at, PAD), :].astype(jnp.bfloat16)
        return carry

    lax.fori_loop(POLE, POLE + 128, narrow, 0, unroll=4)
    rows_ref[POLE + 128 :] = jnp.zeros((POLE, PAD, 128), jnp.bfloat16)

    pl.semaphore_wait(barrier, LINE + PLANE - 2)
    for d in range(1, LINE):
        pl.semaphore_signal(
            ready_sem, inc=1, device_id=at_line(lax.rem(me + d, LINE)), device_id_type=MESH
        )

    caps = [
        remote(
            rows_ref.at[POLE + g], rows_ref.at[POLE - 1 - g], cap_send.at[g], cap_recv.at[g],
            (lax.rem(y + 2, 4), z, xlo, chan),
        )
        for g in range(POLE)
    ]
    for copy in caps:
        copy.start()

    other = lax.rem(chan + 2, 4)
    twin = chan + 1 - 2 * lax.rem(chan, 2)
    part_spot = lambda p: pl.ds(pl.multiple_of(p * C, 128), C)
    owned = y + 4 * z
    piece = part_spot(lax.rem(owned, K))
    across = remote(
        weight_ref.at[:, piece], whole_ref.at[chan, :, piece], part_send, part_recv, (y, z, 1 - xlo, other)
    )

    @pl.when(owned < K)
    def _():
        across.start()

    def line_copy(peer, c):
        return remote(
            rows_ref.at[pl.ds(peer * ROWS + 4 * c, 4)], got_ref.at[me, pl.ds(4 * c, 4)],
            line_send.at[c], line_recv.at[c], at_line(peer),
        )

    def line_all(c, count):
        both = got_ref.at[pl.ds(0, count), pl.ds(0, 4)]
        return remote(both, both, line_send.at[c], line_recv.at[c], at_line(lax.rem(me + 1, LINE)))

    def takes(peer, c):
        return lax.rem(peer, 2) * 2 + 4 > c

    def each_line(c, act):
        for d in range(1, LINE):
            peer = lax.rem(me + d, LINE)
            if isinstance(c, int) and c < 4:
                act(peer)
            else:
                pl.when(takes(peer, c))(functools.partial(act, peer))

    for d in range(1, LINE):
        peer = lax.rem(me + d, LINE)

        @pl.when(peer != 0)
        def _():
            line_copy(peer, 0).start()

    each_line(1, lambda peer: line_copy(peer, 1).start())

    def advance(c):
        line_all(c - 2, LINE - 1).wait_send()
        each_line(c, lambda peer: line_copy(peer, c).start())

    mine = pltpu.make_async_copy(weight_ref, whole_ref.at[chan], own_sem.at[0])
    mine.start()
    to_twin = remote(weight_ref, whole_ref.at[chan], pair_send.at[0], pair_recv.at[0], (y, z, xlo, twin))
    to_twin.start()

    for copy in caps:
        copy.wait()

    @pl.when(me != 0)
    def _():
        line_copy(0, 0).start()

    own = pltpu.make_async_copy(
        rows_ref.at[pl.ds(me * ROWS, SPAN)], got_ref.at[me], own_sem.at[1]
    )
    own.start()
    for copy in loads:
        copy.wait()

    def one_filter(k, carry):
        for e in range(NNZ):
            tall = jnp.concatenate(
                [basis_ref[e, k], jnp.zeros((128 - 65, 128), jnp.float32)], axis=0
            )
            tmp_ref[e] = tall.T
        for e in range(NNZ):
            taps = tmp_ref[e, pl.ds(pl.multiple_of(me * ROWS, ROWS), ROWS), :]
            filt_ref[pl.ds(e * 16 + k, ROWS, stride=TAPS), :] = taps
        return carry

    lax.fori_loop(0, K, one_filter, 0)
    away = jnp.abs(lax.broadcasted_iota(jnp.int32, (16, 128), 1) - 32)

    def scale(row, carry):
        for e in range(NNZ):
            from_row = src_ref[e, me * ROWS + row]
            quad = quad_ref[jnp.where(from_row < POLE, POLE - 1 - from_row, from_row - POLE)]
            reach = reach_ref[e, me * ROWS + row]
            at = pl.ds(pl.multiple_of(row * TAPS + e * 16, 16), 16)
            kept = jnp.where(away <= reach, filt_ref[at, :] * quad, 0.0)
            filt_ref[at, :] = kept.astype(jnp.bfloat16).astype(jnp.float32)
        return carry

    lax.fori_loop(0, ROWS, scale, 0)

    def fan_z(target):
        return remote(
            whole_ref.at[other, :, piece], whole_ref.at[other, :, piece],
            fan_z_send.at[target], fan_z_recv.at[z], (y, target, xlo, chan),
        )

    @pl.when(owned < K)
    def _():
        across.wait()
        for d in range(1, 4):
            fan_z(lax.rem(z + d, 4)).start()

    advance(2)

    def fan_y(j, target):
        at = whole_ref.at[other, :, part_spot(y + 4 * j)]
        return remote(at, at, fan_y_send.at[j, target], fan_y_recv.at[y, j], (target, z, xlo, chan))

    def fan_y_from(start, j):
        at = whole_ref.at[other, :, start * C + 4 * j * C : start * C + 4 * j * C + C]
        return remote(at, at, fan_y_send.at[j, start], fan_y_recv.at[start, j], (start, z, xlo, chan))

    def each_piece(act):
        for j in range(3):
            if j < 2:
                act(j)
            else:
                pl.when(y == 0)(functools.partial(act, j))

    def pass_on(j):
        at = whole_ref.at[other, :, part_spot(y + 4 * j)]

        @pl.when(z != j)
        def _():
            remote(at, at, fan_z_send.at[0], fan_z_recv.at[j], (y, j, xlo, chan)).wait_recv()

        for d in range(1, 4):
            fan_y(j, lax.rem(y + d, 4)).start()

    each_piece(pass_on)
    advance(3)

    def one_table(b, carry):
        at = pl.multiple_of(b * 96, 96)
        part = u_ref[pl.ds(b, 1), :] * p_ref[...] + v_ref[pl.ds(b, 1), :] * q_ref[...]
        table_ref[pl.ds(at, 96), :] = part.astype(jnp.bfloat16)
        return carry

    lax.fori_loop(0, PLANE, one_table, 0)


    def halo_copy(side, c):
        target = lax.rem(yz + PLANE - 1 + 2 * side, PLANE)
        return remote(
            edge_ref.at[side, pl.ds(4 * c, 4)], halo_ref.at[side, pl.ds(4 * c, 4)],
            halo_send.at[c], halo_recv.at[c], at_plane(target),
        )

    def halo_both(c):
        both = halo_ref.at[:, pl.ds(0, 4)]
        return remote(both, both, halo_send.at[c], halo_recv.at[c], at_plane(lax.rem(yz + 1, PLANE)))

    def joined(first, u):
        return jnp.concatenate(
            [got_ref[first + q, u].astype(jnp.float32)[:, :OWN] for q in range(4)], axis=1
        )

    def arrive(c):
        line_all(c, LINE - 1).wait_recv()

        def one(i, carry):
            u = 4 * c + i
            left, right = joined(0, u), joined(4, u)
            edge_ref[0, u] = left[:32].astype(jnp.bfloat16)
            edge_ref[1, u] = right[16:].astype(jnp.bfloat16)
            flat_ref[u, 32:77, :] = left[:SLAB]
            flat_ref[u, 77:122, :] = right[3:]
            return carry

        lax.fori_loop(0, 4, one, 0)
        for side in range(2):
            halo_copy(side, c).start()

    def finish(c):
        halo_both(c).wait_recv()

        def one(i, carry):
            u = 4 * c + i
            flat_ref[u, 0:32, :] = halo_ref[1, u].astype(jnp.float32)
            flat_ref[u, 122:154, :] = halo_ref[0, u].astype(jnp.float32)
            flat_ref[u, 154:EXT, :] = jnp.zeros((EXT - 154, C), jnp.float32)
            x_ref[u] = flat_ref[u].astype(jnp.bfloat16)
            return carry

        lax.fori_loop(0, 4, one, 0)

    twin_copy = remote(
        x_ref.at[pl.ds(0, 8)], land_ref, pair_send.at[2], pair_recv.at[2], (y, z, xlo, twin)
    )

    def late(c):
        @pl.when(odd)
        def _():
            finish(c)

        @pl.when(jnp.logical_not(odd) & (c == 4))
        def _():
            twin_copy.wait_recv()

        @pl.when(jnp.logical_not(odd))
        def _():
            def one(i, carry):
                x_ref[4 * c + i] = land_ref[4 * c - 16 + i]
                return carry

            lax.fori_loop(0, 4, one, 0)

    far_copy = remote(
        whole_ref.at[other], whole_ref.at[other], pair_send.at[1], pair_recv.at[1], (y, z, xlo, twin)
    )
    odd = lax.rem(me, 2) == 1
    own.wait()
    arrive(0)
    advance(4)
    arrive(1)
    arrive(2)
    advance(5)
    arrive(3)

    @pl.when(odd)
    def _():
        arrive(4)

    for start in range(4):
        for j in range(3 if start == 0 else 2):

            @pl.when(y != start)
            def _():
                fan_y_from(start, j).wait_recv()

    far_copy.start()
    for c in range(3):
        finish(c)

    @pl.when(odd)
    def _():
        twin_copy.start()

    lane = lax.broadcasted_iota(jnp.int32, (TILE, 128), 1)

    def build(row, band_ref):
        for k in range(K):
            turned = []
            for e in range(NNZ):
                taps = filt_ref[pl.ds(row * TAPS + e * 16 + k, 1), :]
                spread = jnp.broadcast_to(taps, (TILE, 128))
                turned.append(pltpu.roll(spread, 96 * e % 128, 1, stride=1, stride_axis=0))
            tiles = [
                jnp.where(lane < 96, turned[0], turned[1]),
                jnp.where(lane < 64, turned[1], turned[2]),
                jnp.where(lane < 32, turned[2], turned[3]),
                turned[4],
            ]
            for t in range(4):
                band_ref[k * TILE : (k + 1) * TILE, t * 128 : (t + 1) * 128] = tiles[t].astype(jnp.bfloat16)

    def convolve(row, band_ref):
        sources = [jnp.clip(src_ref[e, me * ROWS + row] - me * ROWS, 0, SPAN - 1) for e in range(NNZ)]
        windows = []
        for b in range(3):
            pieces = [x_ref[u, b * TILE : b * TILE + 96, :] for u in sources]
            windows.append(jnp.concatenate(pieces + [x_ref[sources[0], 0:32, :]], axis=0))
        total = jnp.dot(
            band_ref[...], jnp.concatenate(windows, axis=1), preferred_element_type=jnp.float32
        )
        rounded = total.astype(jnp.bfloat16)
        for b in range(3):
            at = pl.multiple_of(lax.rem(row, 4) * 96 + b * TILE, TILE)
            for k in range(K):
                filtered_ref[pl.ds(at, TILE), k * C : (k + 1) * C] = rounded[
                    k * TILE : (k + 1) * TILE, b * C : (b + 1) * C
                ]

    ty, tz = me // 2, lax.rem(me, 2) * 2

    def to_self(s, o):
        return (ty == y) & (tz + s // 2 == z) & (lax.rem(s, 2) == xlo) & (chan == o)

    def send_copy(s, o):
        return remote(
            sent_ref.at[s, o], all_ref.at[yz], send_sem, recv_sem,
            (ty, tz + s // 2, lax.rem(s, 2), o),
        )

    def own_copy(s, o):
        return pltpu.make_async_copy(sent_ref.at[s, o], all_ref.at[yz], own_sem.at[2])

    build(0, even_ref)

    def pair(p, carry):
        c = p // 2

        @pl.when(p == 2)
        def _():
            finish(3)

        @pl.when((lax.rem(p, 2) == 0) & (p > 2))
        def _():
            late(c + 2)

        convolve(2 * p, even_ref)
        build(2 * p + 1, odd_ref)
        convolve(2 * p + 1, odd_ref)
        build(jnp.minimum(2 * p + 2, ROWS - 1), even_ref)

        @pl.when((p == 0) & odd)
        def _():
            arrive(5)

        @pl.when(p == 1)
        def _():
            far_copy.wait()
            to_twin.wait()
            pl.semaphore_wait(ready_sem, LINE - 1)
            mine.wait()

        @pl.when(lax.rem(p, 2) == 1)
        def _():
            acc = lax.dot_general(
                filtered_ref[...],
                whole_ref[...].reshape(C, K * C),
                (((1,), (1,)), ((), ())),
                preferred_element_type=jnp.float32,
            )
            for o in range(4):
                joint = jnp.concatenate(
                    [acc[i * 96 : (i + 1) * 96, o * OWN : (o + 1) * OWN] for i in range(4)], axis=1
                )
                sent_ref[c, o] = joint.astype(jnp.bfloat16)
            for o in range(4):

                @pl.when(to_self(c, o))
                def _():
                    own_copy(c, o).start()

                @pl.when(jnp.logical_not(to_self(c, o)))
                def _():
                    send_copy(c, o).start()

        return carry

    lax.fori_loop(0, 8, pair, 0)

    def final(count):
        both = all_ref.at[pl.ds(0, count)]
        return remote(both, both, send_sem, recv_sem, at_line(lax.rem(me + 1, LINE)))

    @pl.when(source == me)
    def _():
        own_copy(0, 0).wait()
        final(PLANE - 1).wait_send()

    @pl.when(source != me)
    def _():
        final(PLANE).wait_send()

    for c in range(4):
        halo_both(c).wait_send()
    for c in (4, 5):

        @pl.when(odd)
        def _():
            halo_both(c).wait_send()
            line_all(c, 3).wait_send()

        @pl.when(jnp.logical_not(odd))
        def _():
            line_all(c, 4).wait_send()

    @pl.when(odd)
    def _():
        twin_copy.wait_send()

    @pl.when(owned < K)
    def _():
        for d in range(1, 4):
            fan_z(lax.rem(z + d, 4)).wait_send()

    def left(j):
        for d in range(1, 4):
            fan_y(j, lax.rem(y + d, 4)).wait_send()

    each_piece(left)

    @pl.when(source == me)
    def _():
        final(PLANE - 1).wait_recv()

    @pl.when(source != me)
    def _():
        final(PLANE).wait_recv()

    result = lax.dot_general(
        all_ref[...].reshape(PLANE * 96, C),
        table_ref[...],
        (((0,), (0,)), ((), ())),
        preferred_element_type=jnp.float32,
    )
    for t in range(12):
        result_ref[t * C : (t + 1) * C, :] = result[:, 128 * t : 128 * (t + 1)]

    def out_copy(g):
        at = pl.ds(45 * g, 45)
        return pltpu.make_async_copy(stage_ref.at[at], out_ref.at[at], out_sem)

    def store(g, carry):
        tiles = []
        for j in range(8):
            tiles.append([result_ref[pl.ds(t * C + 8 * g + j, 4, stride=OWN), :] for t in range(12)])
        flat = []
        for half in range(2):
            pieces = []
            for j in range(4):
                pieces += tiles[4 * half + j][:11] + [tiles[4 * half + j][11][:, :32]]
            four = jnp.concatenate(pieces, axis=1)
            flat += [four[:, 128 * t : 128 * (t + 1)] for t in range(45)]
        for t in range(45):
            stage_ref[45 * g + t] = jnp.concatenate(flat[2 * t : 2 * t + 2], axis=0)
        out_copy(g).start()
        return carry

    lax.fori_loop(0, OWN // 8, store, 0)
    pltpu.make_async_copy(stage_ref, out_ref, out_sem).wait()


def layer(src, reach, quads, fields, weight, basis, tables):
    vmem = pl.BlockSpec(memory_space=pltpu.VMEM)
    smem = pl.BlockSpec(memory_space=pltpu.SMEM)
    dma = pltpu.SemaphoreType.DMA
    wide = 128 + 2 * POLE
    bf16 = jnp.bfloat16
    return pl.pallas_call(
        layer_kernel,
        out_shape=jax.ShapeDtypeStruct((OWN * MODES // 128, 8, 128), jnp.float32),
        in_specs=[smem] * 3 + [vmem] * 2 + [pl.BlockSpec(memory_space=pl.ANY)] * 5,
        out_specs=pl.BlockSpec(memory_space=pl.ANY),
        scratch_shapes=[
            *[pltpu.VMEM(a.shape, a.dtype) for a in (basis, *tables)],
            dma((5,)),
            pltpu.VMEM((OWN * PAD, 128), jnp.float32),
            pltpu.VMEM((wide * PAD, 128), jnp.float32),
            pltpu.VMEM((wide, PAD, 128), bf16),
            pltpu.VMEM((NNZ, 128, 128), jnp.float32),
            pltpu.VMEM((LINE, SPAN, PAD, 128), bf16),
            pltpu.VMEM((2, SPAN, 32, C), bf16),
            pltpu.VMEM((2, SPAN, 32, C), bf16),
            pltpu.VMEM((8, EXT, C), bf16),
            pltpu.VMEM((4, OWN, K * C), bf16),
            pltpu.VMEM((ROWS * TAPS, 128), jnp.float32),
            pltpu.VMEM((SPAN, EXT, C), jnp.float32),
            pltpu.VMEM((SPAN, EXT, C), bf16),
            pltpu.VMEM((K * TILE, 512), bf16),
            pltpu.VMEM((K * TILE, 512), bf16),
            pltpu.VMEM((4 * 96, K * C), bf16),
            pltpu.VMEM((4, 4, 96, C), bf16),
            pltpu.VMEM((PLANE, 96, C), bf16),
            pltpu.VMEM((PLANE * 96, 1536), bf16),
            pltpu.VMEM((12 * C, 128), jnp.float32),
            dma((PARTS,)), dma((PARTS,)), dma((POLE,)), dma((POLE,)), dma((PARTS,)), dma((PARTS,)),
            dma, dma, dma((3,)), dma((3,)), dma((4,)), dma((4,)), dma((3, 4)), dma((4, 3)), dma((3,)),
            dma, dma, pltpu.SemaphoreType.REGULAR,
            pltpu.VMEM((OWN * MODES // 128, 8, 128), jnp.float32), dma,
        ],
        compiler_params=pltpu.CompilerParams(
            collective_id=0, has_side_effects=True, vmem_limit_bytes=60 << 20
        ),
    )(src, reach, quads, fields, weight, basis, *tables)


def dft_parts():
    modes = np.arange(MODES)
    high = 2 * math.pi * ((np.arange(PLANE)[:, None] * WIDTH * modes[None]) % NLON) / NLON
    low = 2 * math.pi * ((np.arange(96)[:, None] * modes[None]) % NLON) / NLON
    factor = 1 / math.sqrt(NLON)
    inside = (np.arange(96) < WIDTH)[:, None]
    ca, sa = np.cos(high) * factor, np.sin(high) * factor
    cb, sb = np.cos(low) * inside, np.sin(low) * inside
    side = lambda a, b: jnp.asarray(np.concatenate([a, b, 0 * a[:, :96]], axis=1), jnp.float32)
    return side(cb, cb), side(sb, sb), side(ca, -sa), side(-sa, -ca)


def shards(fields, mix_weight, basis_values, source_rows, lon_reach, quad_weights):
    out = layer(
        source_rows.T, lon_reach.T, quad_weights, fields, mix_weight, basis_values, dft_parts()
    )
    out = out.reshape(OWN * 2 * MODES // 128, 4, 128)
    return out.transpose(1, 0, 2).reshape(4, OWN * 2 * MODES)


def solution(mesh):
    fine = Mesh(mesh.devices.reshape(4, 4, 2, 4), ("y", "z", "xlo", "chan"))
    lon = ("y", "z", "xlo")
    placed = (P(lon, "chan"), P("chan", None), P(), P(), P(), P())
    return jax.shard_map(
        shards, mesh=fine, in_specs=placed, out_specs=P(lon, "chan"), check_vma=False
    )
```
